512 devices in a mesh: row: 16 (over y, core), col: 32 (over z, x).
Axes of the slice: x: 4, y: 8, z: 8, core: 2. Of those that a mesh axis runs over, the one named last changes fastest.
Arguments:
- row_points: bfloat16 [64, 4096], P(None, 'row'), may hold values from -6 to 6
- col_points: bfloat16 [64, 262144], P(None, 'col'), may hold values from -6 to 6
- random_panel: bfloat16 [262144, 128], P('col'), may hold values from -6 to 6
Outputs:
- left_basis: float32 [4096, 128], P('row')
- coefficients: bfloat16 [128, 262144], P('row', 'col')
The draws below stay inside these ranges and needn't reach their ends.
All inputs are finite; a program needn't handle non-finite values.
Results may differ from the reference program's by a relative error of at most 0.015.
Values may be sent and summed in bfloat16 or wider, within the bound.
A program may use at most 64 MiB of HBM per device.

```python
import math
import jax
import jax.numpy as jnp
from jax import lax

DIM = 64
RANK = 128
ROWS = 4096
COLS = 262144


def block_scale(stream_key, extent, shards, smallest, high):
    def one(axis_at, blocks):
        heights = jax.random.uniform(jax.random.fold_in(jax.random.fold_in(stream_key, 6), axis_at), (blocks,), jnp.float32, smallest / len(shards), high / len(shards))
        return jnp.repeat(jnp.exp(heights), extent[axis_at] // blocks).reshape((-1,) + (1,) * (len(extent) - axis_at - 1))

    factor_of = one(*shards[0])
    for cut in shards[1:]:
        factor_of = factor_of * one(*cut)
    return factor_of


def noise(rng, extent, spread, limit, cuts=(), kind=jnp.bfloat16):
    level = block_scale(rng, extent, cuts, -0.22, 0.18) if cuts else 1.0
    entries = jax.random.normal(rng, extent, jnp.float32) * spread * level
    return jnp.minimum(jnp.maximum(entries, -limit), limit).astype(kind)


def setup_inputs(seed: int = 0) -> dict:
    key_of = jax.random.split(jax.random.key(seed), 4)
    return {
        "row_points": noise(key_of[0], (DIM, ROWS), 1.0, 6.0, ((1, 16),)),
        "col_points": noise(key_of[1], (DIM, COLS), 1.0, 6.0, ((1, 32),)),
        "random_panel": noise(key_of[2], (COLS, RANK), 1.0, 6.0, ((0, 32),)),
    }


def kernel_tile(points_left, left_sq, col_block):
    cross = jnp.dot(points_left.T.astype(jnp.float32), col_block.astype(jnp.float32), preferred_element_type=jnp.float32)
    col_sq = lax.optimization_barrier(jnp.sum(jnp.square(col_block.astype(jnp.float32)), axis=0))
    exp_scale = 2.0 / DIM
    return jnp.exp((2.0 * cross - left_sq[:, None] - col_sq[None, :]) * exp_scale)

def reference(row_points, col_points, random_panel):
    block_width = math.gcd(COLS, 4096)
    block_count = COLS // block_width
    row_sq = lax.optimization_barrier(jnp.sum(jnp.square(row_points.astype(jnp.float32)), axis=0))
    blocks = col_points.reshape(DIM, block_count, block_width).transpose(1, 0, 2)
    panel_blocks = random_panel.reshape(block_count, block_width, RANK)

    def add_block(accum_sum, block_pair):
        col_block, panel_block = block_pair
        kernel = kernel_tile(row_points, row_sq, col_block).astype(jnp.bfloat16)
        return (accum_sum + jnp.dot(kernel.astype(jnp.float32), panel_block.astype(jnp.float32), preferred_element_type=jnp.float32), None)
    sketch, _ = lax.scan(add_block, jnp.zeros((ROWS, RANK), jnp.float32), (blocks, panel_blocks))
    gram_matrix = jnp.dot(sketch.T.astype(jnp.float32), sketch.astype(jnp.float32), precision=lax.Precision.HIGHEST, preferred_element_type=jnp.float32)
    factor = jnp.linalg.cholesky(gram_matrix)
    orthonormal = jax.scipy.linalg.solve_triangular(factor, sketch.T, lower=True).T
    left_basis = orthonormal * math.sqrt(ROWS)
    orth_bf = orthonormal.astype(jnp.bfloat16)

    def project(col_block):
        kernel = kernel_tile(row_points, row_sq, col_block).astype(jnp.bfloat16)
        return jnp.dot(orth_bf.T.astype(jnp.float32), kernel.astype(jnp.float32), preferred_element_type=jnp.float32).astype(jnp.bfloat16)
    pieces = lax.map(project, blocks)
    coefficients = pieces.transpose(1, 0, 2).reshape(RANK, COLS)
    return (left_basis, coefficients)
```

```python
import functools
import math

import jax
import jax.numpy as jnp
from jax import lax
from jax.experimental import pallas as pl
from jax.experimental.pallas import tpu as pltpu
from jax.sharding import PartitionSpec as P

MESH = pl.DeviceIdType.MESH
F32 = jnp.float32
BF16 = jnp.bfloat16
HIGH = lax.Precision.HIGHEST
STAGES = 11
RS, AGC, SY, SZ, SX, RPY, TX, GRS, GAG, SZF, SXF = range(STAGES)
A2A = STAGES
DEPTH = 128


def dot(a, b, ca, cb, precision=None):
    return lax.dot_general(
        a, b, (((ca,), (cb,)), ((), ())), precision=precision, preferred_element_type=F32
    )


def ring(n):
    return sorted(range(n), key=lambda k: -min(k, n - k))


def plane(a, b):
    far = lambda k, n: min(k, n - k)
    both = [(i, j) for i in range(a) for j in range(b) if i or j]
    return sorted(both, key=lambda o: -(far(o[0], a) + far(o[1], b)))


def split3(v):
    hi = v.astype(BF16).astype(F32)
    mid = (v - hi).astype(BF16).astype(F32)
    return hi, mid, v - hi - mid


def split2(v):
    hi = v.astype(BF16)
    return hi, (v - hi.astype(F32)).astype(BF16)


def inverse_factor(gram, block=32, inner=16):
    n = gram.shape[0]
    count, tiles = n // block, block // 8
    lane = lax.broadcasted_iota(jnp.int32, (8, n), 1)
    sub = lax.broadcasted_iota(jnp.int32, (8, n), 0)
    rows = [gram[8 * t : 8 * t + 8] for t in range(n // 8)]
    for b in range(count):
        base = b * block
        p = rows[b * tiles : (b + 1) * tiles]
        col = [None] * block
        diag = [None] * tiles
        for i in range(block):
            ti, si = i // 8, i % 8
            at = lane == base + i
            stop = (i // inner + 1) * inner
            if i % inner == 0:
                for j in range(i, stop):
                    k = base + j
                    col[j] = [
                        jnp.broadcast_to(p[t][:, k : k + 1], (8, n)) if t >= j // 8 else None
                        for t in range(tiles)
                    ]
            d = jnp.broadcast_to(col[i][ti][si : si + 1], (8, n))
            diag[ti] = d if diag[ti] is None else jnp.where(sub == si, d, diag[ti])
            inv = 1.0 / d
            m = [None] * tiles
            for t in range(ti, tiles):
                m[t] = col[i][t] * inv
            m[ti] = jnp.where(sub > si, m[ti], 0.0)
            for j in range(i + 1, stop):
                e = jnp.broadcast_to(col[i][j // 8][j % 8 : j % 8 + 1], (8, n))
                for t in range(j // 8, tiles):
                    col[j][t] = col[j][t] - m[t] * e
            row = jnp.where(at, 1.0, jnp.broadcast_to(p[ti][si : si + 1], (8, n)))
            for t in range(ti, tiles):
                keep = (sub == si).astype(F32) if t == ti else 0.0
                p[t] = jnp.where(at, keep, p[t]) - m[t] * row
        for t in range(tiles):
            dead = (lane > sub + (base + 8 * t)) & (lane < base + block)
            p[t] = jnp.where(dead, 0.0, p[t] * lax.rsqrt(diag[t]))
            rows[b * tiles + t] = p[t]
        if b + 1 < count:
            panel = jnp.concatenate(p, axis=0)
            turned = panel.T
            inside = (lane >= base) & (lane < base + block)
            for u in range(b + 1, count):
                upd = dot(turned[u * block : (u + 1) * block], panel, 1, 0, HIGH)
                for t in range(tiles):
                    at = u * tiles + t
                    rows[at] = jnp.where(inside, 0.0, rows[at]) - upd[8 * t : 8 * t + 8]
    rows = [jnp.where(lane > sub + 8 * t, 0.0, rows[t]) for t in range(n // 8)]
    return jnp.concatenate(rows, axis=0)


def body(
    nrow, ncol, nx, chunk,
    rp_hbm, col_hbm, panel_hbm, left_ref, coef_ref,
    rp, caug, panel, part, rs_buf, srow, sy, sg, rpb, rpt, k2, gpart, grs, gfull, tsum, ts, tr,
    cs, cr,
    send, recv, in_sem,
):
    dim, rows = rp.shape
    cols, rank = panel.shape
    nz, ny = ncol // nx, nrow // 2
    ch = rows // ncol
    gch = rank // nrow
    own_cols = cols // nrow
    chunks = cols // chunk
    scale = 4.0 / dim
    r, c = lax.axis_index("row"), lax.axis_index("col")
    y, core = r // 2, lax.rem(r, 2)
    z, x = c // nx, lax.rem(c, nx)
    partner = y * 2 + 1 - core

    def load(j):
        at = pl.ds(pl.multiple_of(j * chunk, chunk), chunk)
        return (
            pltpu.make_async_copy(col_hbm.at[:, at], caug.at[pl.ds(0, dim), at], in_sem.at[0, j]),
            pltpu.make_async_copy(panel_hbm.at[at, :], panel.at[at, :], in_sem.at[1, j]),
        )

    def put(stage, src, dst, row, col):
        pltpu.make_async_remote_copy(
            src_ref=src, dst_ref=dst, send_sem=send.at[stage], recv_sem=recv.at[stage],
            device_id=(row, col), device_id_type=MESH,
        ).start()

    def landed(stage, ref):
        pltpu.make_async_copy(ref, ref, recv.at[stage]).wait()

    def left_us(stage, ref):
        pltpu.make_async_copy(ref, ref, send.at[stage]).wait()

    def col_at(dz, dx):
        return lax.rem(z + dz, nz) * nx + lax.rem(x + dx, nx)

    def row_at(dy, dc):
        return lax.rem(y + dy, ny) * 2 + (1 - core if dc else core)

    near_z = [k for k in ring(nz) if 0 < min(k, nz - k) <= max(1, nz // 4)]
    far_z = [k for k in ring(nz) if min(k, nz - k) > max(1, nz // 4)]

    def stage_z(k):
        return SZ if k in near_z else SZF

    barrier = pltpu.get_barrier_semaphore()

    for dz, dx in plane(nz, nx):
        to = (r, col_at(dz, dx))
        pl.semaphore_signal(barrier, inc=1, device_id=to, device_id_type=MESH)
    for dy, dc in plane(ny, 2):
        to = (row_at(dy, dc), c)
        pl.semaphore_signal(barrier, inc=1, device_id=to, device_id_type=MESH)

    first = pltpu.make_async_copy(rp_hbm, rp, in_sem.at[0, chunks])
    first.start()
    for j in range(chunks):
        for copy in load(j):
            copy.start()

    def aug_rows(points):
        p = points.astype(F32)
        n = p.shape[1]
        hi, mid, lo = split3(-0.5 * jnp.sum(p * p, axis=0, keepdims=True))
        i = lax.broadcasted_iota(jnp.int32, (DEPTH - dim, n), 0)
        extra = jnp.where(i == 0, hi, jnp.where(i == 1, mid, jnp.where(i == 2, lo, 0.0)))
        extra = jnp.where((i > 2) & (i < 6), 1.0, extra)
        return jnp.concatenate([p, extra], axis=0).T

    first.wait()
    lhs = aug_rows(rp[...]).astype(BF16)
    step = min(256, chunk)

    @pl.loop(0, chunks)
    def _(j):
        at = pl.ds(pl.multiple_of(j * chunk, chunk), chunk)
        load(j)[0].wait()
        block = caug[0:dim, at].astype(F32)
        hi, mid, lo = split3(-0.5 * jnp.sum(block * block, axis=0, keepdims=True))
        i = lax.broadcasted_iota(jnp.int32, (16, chunk), 0)
        extra = jnp.where(i == 3, hi, jnp.where(i == 4, mid, jnp.where(i == 5, lo, 0.0)))
        caug[dim : dim + 16, at] = jnp.where(i < 3, 1.0, extra).astype(BF16)
        caug[dim + 16 : DEPTH, at] = jnp.zeros((DEPTH - dim - 16, chunk), BF16)

    for j in range(chunks):
        load(j)[1].wait()
    total = jnp.zeros((rows, rank), F32)
    for s in range(cols // step):
        sat = slice(s * step, (s + 1) * step)
        kern = jnp.exp(dot(lhs, caug[:, sat], 1, 0) * scale).astype(BF16)
        total = total + dot(kern, panel[sat, :], 1, 0)
    part[...] = total.reshape(part.shape)

    pl.semaphore_wait(barrier, ncol + nrow - 2)

    for dz, dx in plane(nz, nx):
        to = col_at(dz, dx)
        put(RS, part.at[to], rs_buf.at[dz * nx + dx - 1], r, to)

    for dy in ring(ny):
        if dy:
            put(RPY, rp, rpb.at[y], row_at(dy, 0), c)
    rpb[y] = rp[...]

    landed(RS, rs_buf)
    total = part[c]
    for k in range(ncol - 1):
        total = total + rs_buf[k]
    srow[c] = total
    sy[y] = total
    for dy in ring(ny):
        if dy:
            put(SY, sy.at[y], sy.at[y], row_at(dy, 0), c)
    for dz, dx in plane(nz, nx):
        put(AGC, srow.at[c], srow.at[c], r, col_at(dz, dx))

    landed(SY, sy.at[pl.ds(0, ny - 1)])
    sg[x, z] = sy[...].reshape(ny * ch, rank).astype(BF16)
    for dz in ring(nz):
        if dz:
            put(stage_z(dz), sg.at[x, z], sg.at[x, z], r, col_at(dz, 0))

    landed(AGC, srow.at[pl.ds(0, ncol - 1)])
    sketch = srow[...].reshape(rows, rank)
    gpart[...] = dot(sketch.T, sketch, 1, 0, HIGH).reshape(gpart.shape)
    for dy, dc in plane(ny, 2):
        to = row_at(dy, dc)
        put(GRS, gpart.at[to], grs.at[dy * 2 + dc - 1], to, c)

    landed(RPY, rpb.at[pl.ds(0, ny - 1)])

    @pl.loop(0, ny)
    def _(j):
        t = aug_rows(rpb[j])
        for cc in range(ncol):
            rpt[cc % nx, cc // nx, j] = t[cc * ch : (cc + 1) * ch]

    sides = [1, nx - 1] if nx > 2 else [1]

    def forward(offsets):
        for dz in offsets:
            zz = lax.rem(z + dz, nz)
            for dx in ring(nx):
                if dx:
                    put(SX if dx in sides else SXF, sg.at[x, zz], sg.at[x, zz], r, col_at(0, dx))

    def partial(k):
        return dot(sg[k].reshape(deep, rank), k2[k], 0, 0)

    landed(SZ, sg.at[0, pl.ds(0, len(near_z))])
    forward([0] + near_z)

    deep = nz * ny * ch
    tile = min(512, deep)
    pair = 2 * own_cols

    @pl.loop(0, nx * (deep // tile))
    def _(j):
        jx, js = j // (deep // tile), lax.rem(j, deep // tile)
        zs = nz // (deep // tile)
        p = rpt[jx, pl.ds(js * zs, zs)].reshape(tile, DEPTH).astype(BF16)
        rat = pl.ds(pl.multiple_of(js * tile, tile), tile)
        for s in range(pair // step):
            sat = pl.ds(pl.multiple_of(y * pair + s * step, step), step)
            k2[jx, rat, s * step : (s + 1) * step] = jnp.exp(
                dot(p, caug[:, sat], 1, 0) * scale
            ).astype(BF16)

    landed(GRS, grs)
    gsum = gpart[r]
    for k in range(nrow - 1):
        gsum = gsum + grs[k]
    gfull[r] = gsum
    for dy, dc in plane(ny, 2):
        put(GAG, gfull.at[r], gfull.at[r], row_at(dy, dc), c)
    if far_z:
        landed(SZF, sg.at[0, pl.ds(0, len(far_z))])
        forward(far_z)
    tsum[...] = partial(x)
    landed(SX, sg.at[pl.ds(0, len(sides))])
    for dx in sides:
        tsum[...] += partial(lax.rem(x + dx, nx))
    if nx > 2:
        landed(SXF, sg.at[0])
    for k in (1 - core, core):
        half = pl.ds(pl.multiple_of(k * own_cols, own_cols), own_cols)
        t = tsum[:, half]
        if nx > 2:
            far = lax.rem(x + nx // 2, nx)
            t = t + dot(sg[far].reshape(deep, rank), k2[far, :, half], 0, 0)
        ts[k] = t
        if k is not core:
            for i in range(4):
                at = pl.ds(i * (rank // 4), rank // 4)
                put(TX, ts.at[1 - core, at], tr.at[at], partner, c)
    landed(GAG, gfull.at[pl.ds(0, nrow - 1)])

    inv = inverse_factor(gfull[...].reshape(rank, rank))
    hi, lo = split2(inv)
    inv_wide = jnp.concatenate([hi, hi, lo], axis=1)
    landed(TX, tr)
    hi, lo = split2(ts[core] + tr[...])
    coef = dot(inv_wide, jnp.concatenate([hi, lo, hi], axis=0), 1, 0).astype(BF16)
    for j in range(nrow):
        cs[j] = coef[j * gch : (j + 1) * gch]
    for dy, dc in plane(ny, 2):
        to = row_at(dy, dc)
        put(A2A, cs.at[to], cr.at[r], to, c)
    cr[r] = cs[r]
    left_ref[...] = dot(sketch, inv, 1, 1, HIGH) * math.sqrt(rows * nrow)

    left_us(RS, rs_buf)
    left_us(AGC, srow.at[pl.ds(0, ncol - 1)])
    left_us(SY, sy.at[pl.ds(0, ny - 1)])
    left_us(SZ, sg.at[0, pl.ds(0, len(near_z))])
    if far_z:
        left_us(SZF, sg.at[0, pl.ds(0, len(far_z))])
    left_us(SX, sg.at[pl.ds(0, len(sides))])
    if nx > 2:
        left_us(SXF, sg.at[0])
    left_us(RPY, rpb.at[pl.ds(0, ny - 1)])
    left_us(TX, tr)
    left_us(GRS, grs)
    left_us(GAG, gfull.at[pl.ds(0, nrow - 1)])
    landed(A2A, cr.at[pl.ds(0, nrow - 1)])
    for j in range(nrow):
        coef_ref[:, j * own_cols : (j + 1) * own_cols] = cr[j]
    left_us(A2A, cr.at[pl.ds(0, nrow - 1)])


def per_device(nrow, ncol, nx, row_points, col_points, random_panel):
    dim, rows = row_points.shape
    cols, rank = random_panel.shape
    nz, ny = ncol // nx, nrow // 2
    ch, gch, own_cols = rows // ncol, rank // nrow, cols // nrow
    chunk = min(1024, cols)
    vmem = pl.BlockSpec(memory_space=pltpu.VMEM)
    in_hbm = pl.BlockSpec(memory_space=pltpu.HBM)
    return pl.pallas_call(
        functools.partial(body, nrow, ncol, nx, chunk),
        out_shape=(
            jax.ShapeDtypeStruct((rows, rank), F32),
            jax.ShapeDtypeStruct((gch, cols), BF16),
        ),
        in_specs=[in_hbm] * 3,
        out_specs=(vmem, vmem),
        scratch_shapes=[
            pltpu.VMEM((dim, rows), BF16),
            pltpu.VMEM((DEPTH, cols), BF16),
            pltpu.VMEM((cols, rank), BF16),
            pltpu.VMEM((ncol, ch, rank), F32),
            pltpu.VMEM((ncol - 1, ch, rank), F32),
            pltpu.VMEM((ncol, ch, rank), F32),
            pltpu.VMEM((ny, ch, rank), F32),
            pltpu.VMEM((nx, nz, ny * ch, rank), BF16),
            pltpu.VMEM((ny, dim, rows), BF16),
            pltpu.VMEM((nx, nz, ny, ch, DEPTH), F32),
            pltpu.VMEM((nx, nz * ny * ch, 2 * own_cols), BF16),
            pltpu.VMEM((nrow, gch, rank), F32),
            pltpu.VMEM((nrow - 1, gch, rank), F32),
            pltpu.VMEM((nrow, gch, rank), F32),
            pltpu.VMEM((rank, 2 * own_cols), F32),
            pltpu.VMEM((2, rank, own_cols), F32),
            pltpu.VMEM((rank, own_cols), F32),
            pltpu.VMEM((nrow, gch, own_cols), BF16),
            pltpu.VMEM((nrow, gch, own_cols), BF16),
            pltpu.SemaphoreType.DMA((STAGES + 1,)),
            pltpu.SemaphoreType.DMA((STAGES + 1,)),
            pltpu.SemaphoreType.DMA((2, cols // chunk + 1)),
        ],
        compiler_params=pltpu.CompilerParams(
            collective_id=0, has_side_effects=True, vmem_limit_bytes=67043328 - 10900 * 1024
        ),
    )(*(pltpu.with_memory_space_constraint(v, pltpu.HBM) for v in (row_points, col_points, random_panel)))


def solution(mesh):
    nrow, ncol = mesh.shape["row"], mesh.shape["col"]
    nx = 4 if ncol % 8 == 0 else 2
    return jax.shard_map(
        functools.partial(per_device, nrow, ncol, nx),
        mesh=mesh,
        in_specs=(P(None, "row"), P(None, "col"), P("col", None)),
        out_specs=(P("row", None), P("row", "col")),
        check_vma=False,
    )
```

```python
import functools
import math

import jax
import jax.numpy as jnp
from jax import lax
from jax.experimental import pallas as pl
from jax.experimental.pallas import tpu as pltpu
from jax.sharding import PartitionSpec as P

MESH = pl.DeviceIdType.MESH
F32 = jnp.float32
BF16 = jnp.bfloat16
HIGH = lax.Precision.HIGHEST
STAGES = 11
RS, AGC, SY, SZ, SX, RPY, TX, GRS, GAG, SZF, SXF = range(STAGES)
A2A = STAGES
DEPTH = 128


def dot(a, b, ca, cb, precision=None):
    return lax.dot_general(
        a, b, (((ca,), (cb,)), ((), ())), precision=precision, preferred_element_type=F32
    )


def ring(n):
    return sorted(range(n), key=lambda k: -min(k, n - k))


def plane(a, b):
    far = lambda k, n: min(k, n - k)
    both = [(i, j) for i in range(a) for j in range(b) if i or j]
    return sorted(both, key=lambda o: -(far(o[0], a) + far(o[1], b)))


def split3(v):
    hi = v.astype(BF16).astype(F32)
    mid = (v - hi).astype(BF16).astype(F32)
    return hi, mid, v - hi - mid


def split2(v):
    hi = v.astype(BF16)
    return hi, (v - hi.astype(F32)).astype(BF16)


def inverse_factor(gram, block=32, inner=16):
    n = gram.shape[0]
    count, tiles = n // block, block // 8
    lane = lax.broadcasted_iota(jnp.int32, (8, n), 1)
    sub = lax.broadcasted_iota(jnp.int32, (8, n), 0)
    rows = [gram[8 * t : 8 * t + 8] for t in range(n // 8)]
    for b in range(count):
        base = b * block
        p = rows[b * tiles : (b + 1) * tiles]
        col = [None] * block
        diag = [None] * tiles
        for i in range(0, block, 2):
            ti, si = i // 8, i % 8
            stop = (i // inner + 1) * inner
            if i % inner == 0:
                for j in range(i, stop):
                    k = base + j
                    col[j] = [
                        jnp.broadcast_to(p[t][:, k : k + 1], (8, n)) if t >= j // 8 else None
                        for t in range(tiles)
                    ]

            def at_row(v, k):
                return jnp.broadcast_to(v[k : k + 1], (8, n))

            c1, c2 = col[i], col[i + 1]
            d1, e1, d2 = at_row(c1[ti], si), at_row(c1[ti], si + 1), at_row(c2[ti], si + 1)
            det = d1 * d2 - e1 * e1
            inv1, inv2 = 1.0 / d1, d1 * (1.0 / det)
            diag[ti] = d1 if diag[ti] is None else jnp.where(sub == si, d1, diag[ti])
            diag[ti] = jnp.where(sub == si + 1, det * inv1, diag[ti])
            m1, m2 = [None] * tiles, [None] * tiles
            for t in range(ti, tiles):
                m1[t] = c1[t] * inv1
                if t == ti:
                    m1[t] = jnp.where(sub > si, m1[t], 0.0)
                c2[t] = c2[t] - m1[t] * e1
                m2[t] = c2[t] * inv2
                if t == ti:
                    m2[t] = jnp.where(sub > si + 1, m2[t], 0.0)
            for j in range(i + 2, stop):
                f1, f2 = at_row(c1[j // 8], j % 8), at_row(c2[j // 8], j % 8)
                for t in range(j // 8, tiles):
                    col[j][t] = col[j][t] - m1[t] * f1 - m2[t] * f2
            for m, s in ((m1, si), (m2, si + 1)):
                at = lane == base + 8 * ti + s
                row = jnp.where(at, 1.0, at_row(p[ti], s))
                for t in range(ti, tiles):
                    keep = (sub == s).astype(F32) if t == ti else 0.0
                    p[t] = jnp.where(at, keep, p[t]) - m[t] * row
        for t in range(tiles):
            dead = (lane > sub + (base + 8 * t)) & (lane < base + block)
            p[t] = jnp.where(dead, 0.0, p[t] * lax.rsqrt(diag[t]))
            rows[b * tiles + t] = p[t]
        if b + 1 < count:
            hi, mid, lo = (v.astype(BF16) for v in split3(jnp.concatenate(p, axis=0)))
            stacked = jnp.concatenate([hi, hi, hi, mid, mid, lo], axis=0)
            upd = dot(stacked, jnp.concatenate([hi, mid, lo, hi, mid, hi], axis=0), 0, 0)
            inside = (lane >= base) & (lane < base + block)
            for u in range(b + 1, count):
                for t in range(tiles):
                    at = u * tiles + t
                    rows[at] = jnp.where(inside, 0.0, rows[at]) - upd[8 * at : 8 * at + 8]
    rows = [jnp.where(lane > sub + 8 * t, 0.0, rows[t]) for t in range(n // 8)]
    return jnp.concatenate(rows, axis=0)


def body(
    nrow, ncol, nx, chunk,
    rp_hbm, col_hbm, panel_hbm, left_ref, coef_ref,
    rp, caug, panel, part, rs_buf, srow, sy, sg, rpb, rpt, k2, gpart, grs, gfull, tsum, ts, tr,
    cs, cr,
    send, recv, in_sem,
):
    dim, rows = rp.shape
    cols, rank = panel.shape
    nz, ny = ncol // nx, nrow // 2
    ch = rows // ncol
    gch = rank // nrow
    own_cols = cols // nrow
    chunks = cols // chunk
    scale = 4.0 / dim
    r, c = lax.axis_index("row"), lax.axis_index("col")
    y, core = r // 2, lax.rem(r, 2)
    z, x = c // nx, lax.rem(c, nx)
    partner = y * 2 + 1 - core

    def load(j):
        at = pl.ds(pl.multiple_of(j * chunk, chunk), chunk)
        return (
            pltpu.make_async_copy(col_hbm.at[:, at], caug.at[pl.ds(0, dim), at], in_sem.at[0, j]),
            pltpu.make_async_copy(panel_hbm.at[at, :], panel.at[at, :], in_sem.at[1, j]),
        )

    def put(stage, src, dst, row, col):
        pltpu.make_async_remote_copy(
            src_ref=src, dst_ref=dst, send_sem=send.at[stage], recv_sem=recv.at[stage],
            device_id=(row, col), device_id_type=MESH,
        ).start()

    def landed(stage, ref):
        pltpu.make_async_copy(ref, ref, recv.at[stage]).wait()

    def left_us(stage, ref):
        pltpu.make_async_copy(ref, ref, send.at[stage]).wait()

    def col_at(dz, dx):
        return lax.rem(z + dz, nz) * nx + lax.rem(x + dx, nx)

    def row_at(dy, dc):
        return lax.rem(y + dy, ny) * 2 + (1 - core if dc else core)

    near_z = [k for k in ring(nz) if 0 < min(k, nz - k) <= max(1, nz // 4)]
    far_z = [k for k in ring(nz) if min(k, nz - k) > max(1, nz // 4)]

    def stage_z(k):
        return SZ if k in near_z else SZF

    barrier = pltpu.get_barrier_semaphore()

    for dz, dx in plane(nz, nx):
        to = (r, col_at(dz, dx))
        pl.semaphore_signal(barrier, inc=1, device_id=to, device_id_type=MESH)
    for dy, dc in plane(ny, 2):
        to = (row_at(dy, dc), c)
        pl.semaphore_signal(barrier, inc=1, device_id=to, device_id_type=MESH)

    first = pltpu.make_async_copy(rp_hbm, rp, in_sem.at[0, chunks])
    first.start()
    for j in range(chunks):
        for copy in load(j):
            copy.start()

    def aug_rows(points):
        p = points.astype(F32)
        n = p.shape[1]
        hi, mid, lo = split3(-0.5 * jnp.sum(p * p, axis=0, keepdims=True))
        i = lax.broadcasted_iota(jnp.int32, (DEPTH - dim, n), 0)
        extra = jnp.where(i == 0, hi, jnp.where(i == 1, mid, jnp.where(i == 2, lo, 0.0)))
        extra = jnp.where((i > 2) & (i < 6), 1.0, extra)
        return jnp.concatenate([p, extra], axis=0).T

    first.wait()
    lhs = aug_rows(rp[...]).astype(BF16)
    step = min(256, chunk)

    @pl.loop(0, chunks)
    def _(j):
        at = pl.ds(pl.multiple_of(j * chunk, chunk), chunk)
        load(j)[0].wait()
        block = caug[0:dim, at].astype(F32)
        hi, mid, lo = split3(-0.5 * jnp.sum(block * block, axis=0, keepdims=True))
        i = lax.broadcasted_iota(jnp.int32, (16, chunk), 0)
        extra = jnp.where(i == 3, hi, jnp.where(i == 4, mid, jnp.where(i == 5, lo, 0.0)))
        caug[dim : dim + 16, at] = jnp.where(i < 3, 1.0, extra).astype(BF16)
        caug[dim + 16 : DEPTH, at] = jnp.zeros((DEPTH - dim - 16, chunk), BF16)

    for j in range(chunks):
        load(j)[1].wait()
    total = jnp.zeros((rows, rank), F32)
    for s in range(cols // step):
        sat = slice(s * step, (s + 1) * step)
        kern = jnp.exp(dot(lhs, caug[:, sat], 1, 0) * scale).astype(BF16)
        total = total + dot(kern, panel[sat, :], 1, 0)
    part[...] = total.reshape(part.shape)

    pl.semaphore_wait(barrier, ncol + nrow - 2)

    for dz, dx in plane(nz, nx):
        to = col_at(dz, dx)
        put(RS, part.at[to], rs_buf.at[dz * nx + dx - 1], r, to)

    for dy in ring(ny):
        if dy:
            put(RPY, rp, rpb.at[y], row_at(dy, 0), c)
    rpb[y] = rp[...]

    landed(RS, rs_buf)
    total = part[c]
    for k in range(ncol - 1):
        total = total + rs_buf[k]
    srow[c] = total
    sy[y] = total
    for dy in ring(ny):
        if dy:
            put(SY, sy.at[y], sy.at[y], row_at(dy, 0), c)
    for dz, dx in plane(nz, nx):
        put(AGC, srow.at[c], srow.at[c], r, col_at(dz, dx))

    landed(SY, sy.at[pl.ds(0, ny - 1)])
    sg[x, z] = sy[...].reshape(ny * ch, rank).astype(BF16)
    for dz in ring(nz):
        if dz:
            put(stage_z(dz), sg.at[x, z], sg.at[x, z], r, col_at(dz, 0))

    landed(AGC, srow.at[pl.ds(0, ncol - 1)])
    sketch = srow[...].reshape(rows, rank)
    gpart[...] = dot(sketch.T, sketch, 1, 0, HIGH).reshape(gpart.shape)
    for dy, dc in plane(ny, 2):
        to = row_at(dy, dc)
        put(GRS, gpart.at[to], grs.at[dy * 2 + dc - 1], to, c)

    landed(RPY, rpb.at[pl.ds(0, ny - 1)])

    @pl.loop(0, ny)
    def _(j):
        t = aug_rows(rpb[j])
        for cc in range(ncol):
            rpt[cc % nx, cc // nx, j] = t[cc * ch : (cc + 1) * ch]

    sides = [1, nx - 1] if nx > 2 else [1]

    def forward(offsets):
        for dz in offsets:
            zz = lax.rem(z + dz, nz)
            for dx in ring(nx):
                if dx:
                    put(SX if dx in sides else SXF, sg.at[x, zz], sg.at[x, zz], r, col_at(0, dx))

    def partial(k):
        return dot(sg[k].reshape(deep, rank), k2[k], 0, 0)

    landed(SZ, sg.at[0, pl.ds(0, len(near_z))])
    forward([0] + near_z)

    deep = nz * ny * ch
    tile = min(512, deep)
    pair = 2 * own_cols

    @pl.loop(0, nx * (deep // tile))
    def _(j):
        jx, js = j // (deep // tile), lax.rem(j, deep // tile)
        zs = nz // (deep // tile)
        p = rpt[jx, pl.ds(js * zs, zs)].reshape(tile, DEPTH).astype(BF16)
        rat = pl.ds(pl.multiple_of(js * tile, tile), tile)
        for s in range(pair // step):
            sat = pl.ds(pl.multiple_of(y * pair + s * step, step), step)
            k2[jx, rat, s * step : (s + 1) * step] = jnp.exp(
                dot(p, caug[:, sat], 1, 0) * scale
            ).astype(BF16)

    if far_z:
        landed(SZF, sg.at[0, pl.ds(0, len(far_z))])
        forward(far_z)
    landed(GRS, grs)
    gsum = gpart[r]
    for k in range(nrow - 1):
        gsum = gsum + grs[k]
    gfull[r] = gsum
    for dy, dc in plane(ny, 2):
        put(GAG, gfull.at[r], gfull.at[r], row_at(dy, dc), c)
    tsum[...] = partial(x)
    landed(SX, sg.at[pl.ds(0, len(sides))])
    for dx in sides:
        tsum[...] += partial(lax.rem(x + dx, nx))
    if nx > 2:
        landed(SXF, sg.at[0])
    for k in (1 - core, core):
        half = pl.ds(pl.multiple_of(k * own_cols, own_cols), own_cols)
        t = tsum[:, half]
        if nx > 2:
            far = lax.rem(x + nx // 2, nx)
            t = t + dot(sg[far].reshape(deep, rank), k2[far, :, half], 0, 0)
        ts[k] = t
        if k is not core:
            for i in range(4):
                at = pl.ds(i * (rank // 4), rank // 4)
                put(TX, ts.at[1 - core, at], tr.at[at], partner, c)
    landed(GAG, gfull.at[pl.ds(0, nrow - 1)])

    inv = inverse_factor(gfull[...].reshape(rank, rank))
    hi, lo = split2(inv)
    inv_wide = jnp.concatenate([hi, hi, lo], axis=1)
    landed(TX, tr)
    hi, lo = split2(ts[core] + tr[...])
    coef = dot(inv_wide, jnp.concatenate([hi, lo, hi], axis=0), 1, 0).astype(BF16)
    for j in range(nrow):
        cs[j] = coef[j * gch : (j + 1) * gch]
    for dy, dc in plane(ny, 2):
        to = row_at(dy, dc)
        put(A2A, cs.at[to], cr.at[r], to, c)
    cr[r] = cs[r]
    left_ref[...] = dot(sketch, inv, 1, 1, HIGH) * math.sqrt(rows * nrow)

    left_us(RS, rs_buf)
    left_us(AGC, srow.at[pl.ds(0, ncol - 1)])
    left_us(SY, sy.at[pl.ds(0, ny - 1)])
    left_us(SZ, sg.at[0, pl.ds(0, len(near_z))])
    if far_z:
        left_us(SZF, sg.at[0, pl.ds(0, len(far_z))])
    left_us(SX, sg.at[pl.ds(0, len(sides))])
    if nx > 2:
        left_us(SXF, sg.at[0])
    left_us(RPY, rpb.at[pl.ds(0, ny - 1)])
    left_us(TX, tr)
    left_us(GRS, grs)
    left_us(GAG, gfull.at[pl.ds(0, nrow - 1)])
    landed(A2A, cr.at[pl.ds(0, nrow - 1)])
    for j in range(nrow):
        coef_ref[:, j * own_cols : (j + 1) * own_cols] = cr[j]
    left_us(A2A, cr.at[pl.ds(0, nrow - 1)])


def hand_out(left_in, coef_in, left_out, coef_out, sem):
    copies = [
        pltpu.make_async_copy(left_in, left_out, sem.at[0]),
        pltpu.make_async_copy(coef_in, coef_out, sem.at[1]),
    ]
    for copy in copies:
        copy.start()
    for copy in copies:
        copy.wait()


def per_device(nrow, ncol, nx, row_points, col_points, random_panel):
    dim, rows = row_points.shape
    cols, rank = random_panel.shape
    nz, ny = ncol // nx, nrow // 2
    ch, gch, own_cols = rows // ncol, rank // nrow, cols // nrow
    chunk = min(1024, cols)
    vmem = pl.BlockSpec(memory_space=pltpu.VMEM)
    in_hbm = pl.BlockSpec(memory_space=pltpu.HBM)
    out_hbm = pl.BlockSpec(memory_space=pltpu.HBM)
    found = pl.pallas_call(
        functools.partial(body, nrow, ncol, nx, chunk),
        out_shape=(
            jax.ShapeDtypeStruct((rows, rank), F32),
            jax.ShapeDtypeStruct((gch, cols), BF16),
        ),
        in_specs=[in_hbm] * 3,
        out_specs=(vmem, vmem),
        scratch_shapes=[
            pltpu.VMEM((dim, rows), BF16),
            pltpu.VMEM((DEPTH, cols), BF16),
            pltpu.VMEM((cols, rank), BF16),
            pltpu.VMEM((ncol, ch, rank), F32),
            pltpu.VMEM((ncol - 1, ch, rank), F32),
            pltpu.VMEM((ncol, ch, rank), F32),
            pltpu.VMEM((ny, ch, rank), F32),
            pltpu.VMEM((nx, nz, ny * ch, rank), BF16),
            pltpu.VMEM((ny, dim, rows), BF16),
            pltpu.VMEM((nx, nz, ny, ch, DEPTH), F32),
            pltpu.VMEM((nx, nz * ny * ch, 2 * own_cols), BF16),
            pltpu.VMEM((nrow, gch, rank), F32),
            pltpu.VMEM((nrow - 1, gch, rank), F32),
            pltpu.VMEM((nrow, gch, rank), F32),
            pltpu.VMEM((rank, 2 * own_cols), F32),
            pltpu.VMEM((2, rank, own_cols), F32),
            pltpu.VMEM((rank, own_cols), F32),
            pltpu.VMEM((nrow, gch, own_cols), BF16),
            pltpu.VMEM((nrow, gch, own_cols), BF16),
            pltpu.SemaphoreType.DMA((STAGES + 1,)),
            pltpu.SemaphoreType.DMA((STAGES + 1,)),
            pltpu.SemaphoreType.DMA((2, cols // chunk + 1)),
        ],
        compiler_params=pltpu.CompilerParams(
            collective_id=0, has_side_effects=True, vmem_limit_bytes=67043328 - 10900 * 1024
        ),
    )(
        *(
            pltpu.with_memory_space_constraint(v, pltpu.HBM)
            for v in (row_points, col_points, random_panel)
        )
    )
    return pl.pallas_call(
        hand_out,
        out_shape=tuple(jax.ShapeDtypeStruct(v.shape, v.dtype) for v in found),
        in_specs=[pl.BlockSpec(memory_space=pl.ANY)] * 2,
        out_specs=(out_hbm, out_hbm),
        scratch_shapes=[pltpu.SemaphoreType.DMA((2,))],
        compiler_params=pltpu.CompilerParams(vmem_limit_bytes=1024 * 1024),
    )(*found)


def solution(mesh):
    nrow, ncol = mesh.shape["row"], mesh.shape["col"]
    nx = 4 if ncol % 8 == 0 else 2
    return jax.shard_map(
        functools.partial(per_device, nrow, ncol, nx),
        mesh=mesh,
        in_specs=(P(None, "row"), P(None, "col"), P("col", None)),
        out_specs=(P("row", None), P("row", "col")),
        check_vma=False,
    )
```
